32 devices in a mesh: dp: 4 (over z), ctx: 8 (over y, x, core).
Axes of the slice: x: 2, y: 2, z: 4, core: 2. Of those that a mesh axis runs over, the one named last changes fastest.
Arguments:
- tokens: bfloat16 [4096, 1152], P(('dp', 'ctx')), may hold values from -6 to 6
- in_gain: bfloat16 [1152], P('dp'), may hold values from 0.099609375 to 1.8984375
- query_weight: bfloat16 [1152, 1024], P('dp'), may hold values from -0.1875 to 0.1875
- key_weight: bfloat16 [1152, 256], P('dp'), may hold values from -0.1875 to 0.1875
- value_weight: bfloat16 [1152, 256], P('dp'), may hold values from -0.1875 to 0.1875
- query_gain: bfloat16 [256], P('dp'), may hold values from 0.099609375 to 1.8984375
- key_gain: bfloat16 [256], P('dp'), may hold values from 0.099609375 to 1.8984375
- out_weight: bfloat16 [1024, 1152], P('dp'), may hold values from -0.75 to 0.75
- attn_post_gain: bfloat16 [1152], P('dp'), may hold values from 0.099609375 to 1.8984375
- ffn_pre_gain: bfloat16 [1152], P('dp'), may hold values from 0.099609375 to 1.8984375
- gate_weight: bfloat16 [1152, 6912], P('dp', 'ctx'), may hold values from -0.1875 to 0.1875
- up_weight: bfloat16 [1152, 6912], P('dp', 'ctx'), may hold values from -0.1875 to 0.1875
- down_weight: bfloat16 [1152, 6912], P('dp', 'ctx'), may hold values from -0.078125 to 0.078125
- ffn_post_gain: bfloat16 [1152], P('dp'), may hold values from 0.099609375 to 1.8984375
- cotangent: bfloat16 [4096, 1152], P(('dp', 'ctx')), may hold values from -6 to 6
Outputs:
- block_out: bfloat16 [4096, 1152], P(('dp', 'ctx'))
- input_grad: float32 [4096, 1152], P(('dp', 'ctx'))
- in_gain_grad: float32 [1152], P('dp')
- query_weight_grad: float32 [1152, 1024], P('dp')
- key_weight_grad: float32 [1152, 256], P('dp')
- value_weight_grad: float32 [1152, 256], P('dp')
- query_gain_grad: float32 [256], P('dp')
- key_gain_grad: float32 [256], P('dp')
- out_weight_grad: float32 [1024, 1152], P('dp')
- attn_post_gain_grad: float32 [1152], P('dp')
- ffn_pre_gain_grad: float32 [1152], P('dp')
- gate_weight_grad: float32 [1152, 6912], P('dp', 'ctx')
- up_weight_grad: float32 [1152, 6912], P('dp', 'ctx')
- down_weight_grad: float32 [1152, 6912], P('dp', 'ctx')
- ffn_post_gain_grad: float32 [1152], P('dp')
The draws below stay inside these ranges and needn't reach their ends.
All inputs are finite; a program needn't handle non-finite values.
Results may differ from the reference program's by a relative error of at most 0.017.
Values may be sent and summed in bfloat16 or wider, within the bound.
A program may use at most 128 MiB of HBM per device.

```python
import math
import jax
import jax.numpy as jnp
from jax import lax

D = 1152
HEADS = 4
HEAD = 256
FF = 6912
QWIDTH = 1024
LENGTH = 1024
SEQS = 4
TOKENS = 4096


def steps_of(stream_key, extent, pieces, least, high):
    level, own = 1.0, jax.random.fold_in(stream_key, 6)
    for position, parts in pieces:
        draws = jnp.exp(jax.random.uniform(jax.random.fold_in(own, position), (parts,), jnp.float32, least / len(pieces), high / len(pieces)))
        level = level * jnp.repeat(draws, extent[position] // parts).reshape([-1 if axis == position else 1 for axis in range(len(extent))])
    return level


def normal_values(rng, extent, spread, bound, split=(), held_as=jnp.bfloat16):
    array = spread * jax.random.normal(rng, extent, jnp.float32)
    if split:
        array = array * steps_of(rng, extent, split, -0.22, 0.18)
    return jnp.clip(array, -bound, bound).astype(held_as)


def setup_inputs(seed: int = 0) -> dict:
    key_of = jax.random.split(jax.random.key(seed), 16)
    tokens = normal_values(key_of[0], (TOKENS, D), 1.0, 6.0, ((0, 32),))
    in_gain = jnp.clip(1.0 + 0.18 * jax.random.normal(key_of[1], (D,), jnp.float32), 0.099609375, 1.8984375).astype(jnp.bfloat16)
    query_weight = normal_values(key_of[2], (D, QWIDTH), D ** -0.5, 0.1875, ((0, 4),))
    key_weight = normal_values(key_of[3], (D, HEAD), D ** -0.5, 0.1875, ((0, 4),))
    value_weight = normal_values(key_of[4], (D, HEAD), D ** -0.5, 0.1875, ((0, 4),))
    query_gain = jnp.clip(1.0 + 0.18 * jax.random.normal(key_of[5], (HEAD,), jnp.float32), 0.099609375, 1.8984375).astype(jnp.bfloat16)
    key_gain = jnp.clip(1.0 + 0.18 * jax.random.normal(key_of[6], (HEAD,), jnp.float32), 0.099609375, 1.8984375).astype(jnp.bfloat16)
    out_weight = normal_values(key_of[7], (QWIDTH, D), (QWIDTH // 16) ** -0.5, 0.75, ((0, 4),))
    attn_post_gain = jnp.clip(1.0 + 0.18 * jax.random.normal(key_of[8], (D,), jnp.float32), 0.099609375, 1.8984375).astype(jnp.bfloat16)
    ffn_pre_gain = jnp.clip(1.0 + 0.18 * jax.random.normal(key_of[9], (D,), jnp.float32), 0.099609375, 1.8984375).astype(jnp.bfloat16)
    gate_weight = normal_values(key_of[10], (D, FF), D ** -0.5, 0.1875, ((0, 4), (1, 8)))
    up_weight = normal_values(key_of[11], (D, FF), D ** -0.5, 0.1875, ((0, 4), (1, 8)))
    down_weight = normal_values(key_of[12], (D, FF), FF ** -0.5, 0.078125, ((0, 4), (1, 8)))
    ffn_post_gain = jnp.clip(1.0 + 0.18 * jax.random.normal(key_of[13], (D,), jnp.float32), 0.099609375, 1.8984375).astype(jnp.bfloat16)
    cotangent = normal_values(key_of[14], (TOKENS, D), 1.0, 6.0, ((0, 32),))
    return dict(tokens=tokens, in_gain=in_gain, query_weight=query_weight, key_weight=key_weight, value_weight=value_weight, query_gain=query_gain, key_gain=key_gain, out_weight=out_weight, attn_post_gain=attn_post_gain, ffn_pre_gain=ffn_pre_gain, gate_weight=gate_weight, up_weight=up_weight, down_weight=down_weight, ffn_post_gain=ffn_post_gain, cotangent=cotangent)


EPS = 1e-06
GELU_C = math.sqrt(2.0 / math.pi)
NEG_FILL = -1e+30

def inverse_rms(values):
    return lax.rsqrt(lax.optimization_barrier(jnp.mean(values * values, axis=-1, keepdims=True)) + EPS)

def norm_back(values, scale_inv, gain, grad_out):
    weighted = grad_out * gain
    cubed = scale_inv * scale_inv * scale_inv
    return scale_inv * weighted - values * cubed * lax.optimization_barrier(jnp.mean(weighted * values, axis=-1, keepdims=True))

def gelu_pair(values):
    inner = GELU_C * (values + 0.044715 * values * values * values)
    tanh_val = jnp.tanh(inner)
    result = 0.5 * values * (1.0 + tanh_val)
    slope = 0.5 * (1.0 + tanh_val) + 0.5 * values * (1.0 - tanh_val * tanh_val) * GELU_C * (1.0 + 3.0 * 0.044715 * values * values)
    return (result, slope)

def rotate(values, cosine, sine):
    middle = values.shape[-1] // 2
    first = values[..., :middle]
    second = values[..., middle:]
    return jnp.concatenate([first * cosine - second * sine, second * cosine + first * sine], axis=-1)

def unrotate(grads, cosine, sine):
    middle = grads.shape[-1] // 2
    first = grads[..., :middle]
    second = grads[..., middle:]
    return jnp.concatenate([first * cosine + second * sine, second * cosine - first * sine], axis=-1)

def rope_tables(positions):
    middle = HEAD // 2
    freqs = jnp.exp(-(2.0 * jnp.arange(middle, dtype=jnp.float32) / HEAD) * math.log(1000000.0))
    angles = positions[:, None] * freqs[None, :]
    return (jnp.cos(angles), jnp.sin(angles))

def rounded(values):
    return lax.optimization_barrier(values.astype(jnp.bfloat16)).astype(jnp.float32)

def matmul(left, right):
    return jnp.dot(left, right, preferred_element_type=jnp.float32)

def matmul_tn(left, right):
    return lax.dot_general(left, right, (((0,), (0,)), ((), ())), preferred_element_type=jnp.float32)

def matmul_nt(left, right):
    return lax.dot_general(left, right, (((1,), (1,)), ((), ())), preferred_element_type=jnp.float32)

def reference(tokens, in_gain, query_weight, key_weight, value_weight, query_gain, key_gain, out_weight, attn_post_gain, ffn_pre_gain, gate_weight, up_weight, down_weight, ffn_post_gain, cotangent):
    positions = jnp.arange(LENGTH, dtype=jnp.float32)
    cosine, sine = rope_tables(positions)
    scaling = 1.0 / math.sqrt(HEAD)
    row_index = jnp.arange(LENGTH, dtype=jnp.int32)
    causal = (row_index[:, None] >= row_index[None, :])[None]
    gain_in = in_gain.astype(jnp.float32)
    gain_query = query_gain.astype(jnp.float32)
    gain_key = key_gain.astype(jnp.float32)
    gain_attn = attn_post_gain.astype(jnp.float32)
    gain_pre = ffn_pre_gain.astype(jnp.float32)
    gain_post = ffn_post_gain.astype(jnp.float32)

    def one_sequence(totals, inputs):
        seq_tokens, seq_cot = inputs
        inputs_f = seq_tokens.astype(jnp.float32)
        inv_one = inverse_rms(inputs_f)
        normed_one = (inputs_f * inv_one * gain_in).astype(jnp.bfloat16)
        queries = matmul(normed_one, query_weight).reshape(LENGTH, HEADS, HEAD)
        keys = matmul(normed_one, key_weight)
        values = matmul(normed_one, value_weight).astype(jnp.bfloat16)
        inv_query = inverse_rms(queries)
        inv_key = inverse_rms(keys)
        query_rot = (rotate(queries * inv_query * gain_query, cosine[:, None, :], sine[:, None, :]) * scaling).astype(jnp.bfloat16)
        key_rot = rotate(keys * inv_key * gain_key, cosine, sine).astype(jnp.bfloat16)
        scores = jnp.einsum('qhd,kd->hqk', query_rot.astype(jnp.float32), key_rot.astype(jnp.float32))
        scores = jnp.where(causal, scores, NEG_FILL)
        row_max = lax.optimization_barrier(jnp.max(scores, axis=-1, keepdims=True))
        weights = jnp.where(causal, jnp.exp(scores - row_max), 0.0)
        total = lax.optimization_barrier(jnp.sum(weights, axis=-1, keepdims=True))
        log_total = row_max + jnp.log(total)
        summed = jnp.einsum('hqk,kd->hqd', rounded(weights), values.astype(jnp.float32))
        attn_heads = jnp.transpose(summed / total, (1, 0, 2)).astype(jnp.bfloat16)
        attn_out = attn_heads.reshape(LENGTH, HEADS * HEAD)
        projected = matmul(attn_out, out_weight)
        inv_proj = inverse_rms(projected)
        residual = inputs_f + projected * inv_proj * gain_attn
        inv_two = inverse_rms(residual)
        normed_two = (residual * inv_two * gain_pre).astype(jnp.bfloat16)
        gate = matmul(normed_two, gate_weight)
        upper = matmul(normed_two, up_weight)
        gelu_val, gelu_der = gelu_pair(gate)
        hidden = (gelu_val * upper).astype(jnp.bfloat16)
        ffn_sum = matmul_nt(hidden, down_weight)
        inv_ffn = inverse_rms(ffn_sum)
        block_out = (residual + ffn_sum * inv_ffn * gain_post).astype(jnp.bfloat16)
        cot = seq_cot.astype(jnp.float32)
        grad_post = lax.optimization_barrier(jnp.sum(cot * ffn_sum * inv_ffn, axis=0))
        ffn_sum_grad = norm_back(ffn_sum, inv_ffn, gain_post, cot).astype(jnp.bfloat16)
        hidden_grad = matmul(ffn_sum_grad, down_weight)
        grad_down = matmul_tn(ffn_sum_grad, hidden)
        gate_grad = (hidden_grad * upper * gelu_der).astype(jnp.bfloat16)
        up_grad = (hidden_grad * gelu_val).astype(jnp.bfloat16)
        grad_gate = matmul_tn(normed_two, gate_grad)
        grad_up = matmul_tn(normed_two, up_grad)
        normed_two_grad = matmul_nt(gate_grad, gate_weight) + matmul_nt(up_grad, up_weight)
        grad_pre = lax.optimization_barrier(jnp.sum(normed_two_grad * residual * inv_two, axis=0))
        residual_grad = cot + norm_back(residual, inv_two, gain_pre, normed_two_grad)
        grad_attn = lax.optimization_barrier(jnp.sum(residual_grad * projected * inv_proj, axis=0))
        projected_grad = norm_back(projected, inv_proj, gain_attn, residual_grad).astype(jnp.bfloat16)
        grad_out = matmul_tn(attn_out, projected_grad)
        attn_out_grad = matmul_nt(projected_grad, out_weight).astype(jnp.bfloat16).reshape(LENGTH, HEADS, HEAD)
        delta = lax.optimization_barrier(jnp.sum(attn_out_grad.astype(jnp.float32) * attn_heads.astype(jnp.float32), axis=-1))
        delta = jnp.transpose(delta, (1, 0))[:, :, None]
        probs = jnp.where(causal, jnp.exp(scores - log_total), 0.0)
        prob_grad = jnp.einsum('qhd,kd->hqk', attn_out_grad.astype(jnp.float32), values.astype(jnp.float32))
        score_grad = rounded(probs * (prob_grad - delta))
        values_grad = jnp.einsum('hqk,qhd->kd', rounded(probs), attn_out_grad.astype(jnp.float32))
        key_rot_grad = jnp.einsum('hqk,qhd->kd', score_grad, query_rot.astype(jnp.float32))
        query_rot_grad = jnp.einsum('hqk,kd->qhd', score_grad, key_rot.astype(jnp.float32))
        query_normed_grad = unrotate(query_rot_grad * scaling, cosine[:, None, :], sine[:, None, :])
        grad_qgain = lax.optimization_barrier(jnp.sum(query_normed_grad * queries * inv_query, axis=(0, 1)))
        query_grad = norm_back(queries, inv_query, gain_query, query_normed_grad).reshape(LENGTH, HEADS * HEAD).astype(jnp.bfloat16)
        key_normed_grad = unrotate(key_rot_grad, cosine, sine)
        grad_kgain = lax.optimization_barrier(jnp.sum(key_normed_grad * keys * inv_key, axis=0))
        key_grad = norm_back(keys, inv_key, gain_key, key_normed_grad).astype(jnp.bfloat16)
        value_grad = values_grad.astype(jnp.bfloat16)
        grad_query = matmul_tn(normed_one, query_grad)
        grad_key = matmul_tn(normed_one, key_grad)
        grad_value = matmul_tn(normed_one, value_grad)
        normed_one_grad = matmul_nt(query_grad, query_weight) + matmul_nt(key_grad, key_weight) + matmul_nt(value_grad, value_weight)
        grad_in = lax.optimization_barrier(jnp.sum(normed_one_grad * inputs_f * inv_one, axis=0))
        input_grad = residual_grad + norm_back(inputs_f, inv_one, gain_in, normed_one_grad)
        updates = (grad_in, grad_query, grad_key, grad_value, grad_qgain, grad_kgain, grad_out, grad_attn, grad_pre, grad_gate, grad_up, grad_down, grad_post)
        new_totals = tuple((old + new for old, new in zip(totals, updates)))
        return (new_totals, (block_out, input_grad))
    shapes = (in_gain, query_weight, key_weight, value_weight, query_gain, key_gain, out_weight, attn_post_gain, ffn_pre_gain, gate_weight, up_weight, down_weight, ffn_post_gain)
    initial = tuple((jnp.zeros(item.shape, jnp.float32) for item in shapes))
    seq_inputs = (tokens.reshape(SEQS, LENGTH, D), cotangent.reshape(SEQS, LENGTH, D))
    totals, (outputs, input_grads) = lax.scan(one_sequence, initial, seq_inputs)
    return (outputs.reshape(TOKENS, D), input_grads.reshape(TOKENS, D), totals[0], totals[1], totals[2], totals[3], totals[4], totals[5], totals[6], totals[7], totals[8], totals[9], totals[10], totals[11], totals[12])
```

```python
import functools
import math

import jax
import jax.numpy as jnp
from jax import lax
from jax.experimental import pallas as pl
from jax.experimental.pallas import tpu as pltpu
from jax.sharding import PartitionSpec as P

HEADS = 4
HEAD = 256


EPS = 1e-06
GELU_C = math.sqrt(2.0 / math.pi)
NEG_FILL = -1e30


def inverse_rms(values):
    return lax.rsqrt(jnp.mean(values * values, axis=-1, keepdims=True) + EPS)


def norm_back(values, scale_inv, gain, grad_out):
    weighted = grad_out * gain
    cubed = scale_inv * scale_inv * scale_inv
    return scale_inv * weighted - values * cubed * jnp.mean(
        weighted * values, axis=-1, keepdims=True
    )


def gelu_pair(values):
    inner = GELU_C * (values + 0.044715 * values * values * values)
    tanh_val = jnp.tanh(inner)
    result = 0.5 * values * (1.0 + tanh_val)
    slope = 0.5 * (1.0 + tanh_val) + 0.5 * values * (1.0 - tanh_val * tanh_val) * GELU_C * (
        1.0 + 3.0 * 0.044715 * values * values
    )
    return (result, slope)


def rotate(values, cosine, sine):
    middle = values.shape[-1] // 2
    first = values[..., :middle]
    second = values[..., middle:]
    return jnp.concatenate(
        [first * cosine - second * sine, second * cosine + first * sine], axis=-1
    )


def unrotate(grads, cosine, sine):
    middle = grads.shape[-1] // 2
    first = grads[..., :middle]
    second = grads[..., middle:]
    return jnp.concatenate(
        [first * cosine + second * sine, second * cosine - first * sine], axis=-1
    )


def rope_tables(positions):
    middle = HEAD // 2
    freqs = jnp.exp(-(2.0 * jnp.arange(middle, dtype=jnp.float32) / HEAD) * math.log(1000000.0))
    angles = positions[:, None] * freqs[None, :]
    return (jnp.cos(angles), jnp.sin(angles))


def matmul(left, right):
    return jnp.dot(left, right, preferred_element_type=jnp.float32)


def matmul_tn(left, right):
    return lax.dot_general(
        left, right, (((0,), (0,)), ((), ())), preferred_element_type=jnp.float32
    )


def matmul_nt(left, right):
    return lax.dot_general(
        left, right, (((1,), (1,)), ((), ())), preferred_element_type=jnp.float32
    )


MESH = pl.DeviceIdType.MESH


def swap_kernel(size, axis, kinds, *refs):
    count = len(kinds)
    ins, outs = refs[:count], refs[count : 2 * count]
    send, recv, local = refs[2 * count :]
    me = lax.axis_index(axis)
    barrier = pltpu.get_barrier_semaphore()
    for step in range(1, size):
        peer = lax.rem(me + step, size)
        pl.semaphore_signal(barrier, inc=1, device_id={axis: peer}, device_id_type=MESH)
    pl.semaphore_wait(barrier, size - 1)
    copies = []
    for item, kind in enumerate(kinds):
        for step in range(1, size):
            peer = lax.rem(me + step, size)
            source = ins[item].at[peer] if kind == "swap" else ins[item]
            copy = pltpu.make_async_remote_copy(
                src_ref=source,
                dst_ref=outs[item].at[me],
                send_sem=send.at[item, step - 1],
                recv_sem=recv.at[item, step - 1],
                device_id={axis: peer},
                device_id_type=MESH,
            )
            copy.start()
            copies.append(copy)
    for item, kind in enumerate(kinds):
        source = ins[item].at[me] if kind == "swap" else ins[item]
        copy = pltpu.make_async_copy(source, outs[item].at[me], local.at[item])
        copy.start()
        copies.append(copy)
    for copy in copies:
        copy.wait()


def pair_gather_kernel(size, axis, kinds, *refs):
    count = len(kinds)
    ins, outs = refs[:count], refs[count : 2 * count]
    send, recv, pass_send, pass_recv, local = refs[2 * count :]
    me = lax.axis_index(axis)
    twin = me + 1 - 2 * lax.rem(me, 2)
    half = size // 2
    barrier = pltpu.get_barrier_semaphore()
    for step in range(1, half):
        peer = lax.rem(me + 2 * step, size)
        pl.semaphore_signal(barrier, inc=1, device_id={axis: peer}, device_id_type=MESH)
    pl.semaphore_signal(barrier, inc=1, device_id={axis: twin}, device_id_type=MESH)
    pl.semaphore_wait(barrier, half)
    copies, last = [], []
    for item in range(count):
        row = []
        for step in range(1, half):
            peer = lax.rem(me + 2 * step, size)
            copy = pltpu.make_async_remote_copy(
                src_ref=ins[item],
                dst_ref=outs[item].at[me],
                send_sem=send.at[item, step],
                recv_sem=recv.at[item, step],
                device_id={axis: peer},
                device_id_type=MESH,
            )
            copy.start()
            row.append(copy)
        copies.append(row)
    for item in range(count):
        copy = pltpu.make_async_remote_copy(
            src_ref=ins[item],
            dst_ref=outs[item].at[me],
            send_sem=pass_send.at[item, 0],
            recv_sem=pass_recv.at[item, 0],
            device_id={axis: twin},
            device_id_type=MESH,
        )
        copy.start()
        last.append(copy)
        copy = pltpu.make_async_copy(ins[item], outs[item].at[me], local.at[item])
        copy.start()
        last.append(copy)
    for item in range(count):
        for step in range(1, half):
            copies[item][step - 1].wait_recv()
            origin = lax.rem(me + size - 2 * step, size)
            copy = pltpu.make_async_remote_copy(
                src_ref=outs[item].at[origin],
                dst_ref=outs[item].at[origin],
                send_sem=pass_send.at[item, step],
                recv_sem=pass_recv.at[item, step],
                device_id={axis: twin},
                device_id_type=MESH,
            )
            copy.start()
            last.append(copy)
    for row in copies:
        for copy in row:
            copy.wait_send()
    for copy in last:
        copy.wait()


def exchange(arrays, kinds, axis, size, ident):
    count = len(arrays)
    pairs = all(kind == "gather" for kind in kinds) and axis == "ctx" and size % 2 == 0
    shapes = tuple(
        jax.ShapeDtypeStruct(x.shape if kind == "swap" else (size,) + x.shape, x.dtype)
        for x, kind in zip(arrays, kinds)
    )
    dma = pltpu.SemaphoreType.DMA
    if pairs:
        half = size // 2
        scratch = [dma((count, half))] * 4 + [dma((count,))]
        body = pair_gather_kernel
    else:
        scratch = [dma((count, size - 1))] * 2 + [dma((count,))]
        body = swap_kernel
    moved = sum(x.size * x.dtype.itemsize for x in shapes)
    return pl.pallas_call(
        functools.partial(body, size, axis, tuple(kinds)),
        out_shape=shapes,
        in_specs=[pl.BlockSpec(memory_space=pl.ANY)] * count,
        out_specs=tuple(pl.BlockSpec(memory_space=pl.ANY) for _ in arrays),
        scratch_shapes=scratch,
        compiler_params=pltpu.CompilerParams(collective_id=ident, has_side_effects=True),
        cost_estimate=pl.CostEstimate(flops=0, bytes_accessed=20 * moved, transcendentals=0),
        name=f"exchange_{ident}",
    )(*arrays)


def by_columns(array, parts):
    rows, columns = array.shape
    return jnp.transpose(array.reshape(rows, parts, columns // parts), (1, 0, 2))


def from_columns(array):
    parts, rows, columns = array.shape
    return jnp.transpose(array, (1, 0, 2)).reshape(rows, parts * columns)


def sum_blocks(array):
    return jnp.sum(array.astype(jnp.float32), axis=0)


def on_device(
    dp,
    ctx,
    tokens,
    in_gain,
    query_weight,
    key_weight,
    value_weight,
    query_gain,
    key_gain,
    out_weight,
    attn_post_gain,
    ffn_pre_gain,
    gate_weight,
    up_weight,
    down_weight,
    ffn_post_gain,
    cotangent,
):
    rows, width = tokens.shape
    bf16 = jnp.bfloat16
    scaling = 1.0 / math.sqrt(HEAD)
    ctx_index = lax.axis_index("ctx")
    query_pos = ctx_index * rows + jnp.arange(rows, dtype=jnp.int32)
    cosine, sine = rope_tables(query_pos.astype(jnp.float32))
    gate_full, up_full, down_full = (
        lax.all_gather(gate_weight, "dp", axis=0, tiled=True),
        lax.all_gather(up_weight, "dp", axis=0, tiled=True),
        lax.all_gather(down_weight, "dp", axis=0, tiled=True),
    )

    mixed = jnp.concatenate([query_weight, key_weight, value_weight], axis=1)
    mixed_columns = mixed.shape[1] // ctx
    out_columns = out_weight.shape[1] // ctx
    mixed_slice = lax.dynamic_slice_in_dim(mixed, ctx_index * mixed_columns, mixed_columns, 1)
    out_slice = lax.dynamic_slice_in_dim(out_weight, ctx_index * out_columns, out_columns, 1)
    gains = (in_gain, query_gain, key_gain, attn_post_gain, ffn_pre_gain, ffn_post_gain)
    cuts = [0]
    for gain in gains:
        cuts.append(cuts[-1] + gain.shape[0])
    packed_gains = jnp.concatenate([gain.astype(jnp.float32) for gain in gains])[None]
    mixed_dp, out_dp, gains_dp = exchange(
        (mixed_slice, out_slice, packed_gains), ("gather",) * 3, "dp", dp, 0
    )
    gains_dp = gains_dp[:, 0]
    gain_in, gain_query, gain_key, gain_attn, gain_pre, gain_post = (
        gains_dp[:, low:high].reshape(-1) for low, high in zip(cuts[:-1], cuts[1:])
    )
    mixed_all, out_all, tokens_all = exchange(
        (
            mixed_dp.reshape(-1, mixed_columns),
            out_dp.reshape(-1, out_columns),
            tokens,
        ),
        ("gather",) * 3,
        "ctx",
        ctx,
        1,
    )
    mixed_full = from_columns(mixed_all)
    out_full = from_columns(out_all)
    qwidth = query_weight.shape[1]
    kwidth = key_weight.shape[1]
    query_full = mixed_full[:, :qwidth]
    key_full = mixed_full[:, qwidth : qwidth + kwidth]
    value_full = mixed_full[:, qwidth + kwidth :]

    inputs_f = tokens.astype(jnp.float32)
    inv_one = inverse_rms(inputs_f)
    normed_one = (inputs_f * inv_one * gain_in).astype(bf16)
    all_f = tokens_all.reshape(-1, width).astype(jnp.float32)
    normed_all = (all_f * inverse_rms(all_f) * gain_in).astype(bf16)
    key_pos = jnp.arange(all_f.shape[0], dtype=jnp.int32)
    cosine_all, sine_all = rope_tables(key_pos.astype(jnp.float32))
    queries = matmul(normed_one, query_full).reshape(rows, HEADS, HEAD)
    keys = matmul(normed_one, key_full)
    keys_every = matmul(normed_all, key_full)
    value_all = matmul(normed_all, value_full).astype(bf16)
    inv_query = inverse_rms(queries)
    inv_key = inverse_rms(keys)
    query_rot = (
        rotate(queries * inv_query * gain_query, cosine[:, None, :], sine[:, None, :]) * scaling
    ).astype(bf16)
    key_all = rotate(
        keys_every * inverse_rms(keys_every) * gain_key, cosine_all, sine_all
    ).astype(bf16)
    allowed = (query_pos[:, None] >= key_pos[None, :])[None]
    scores = jnp.einsum("qhd,kd->hqk", query_rot, key_all, preferred_element_type=jnp.float32)
    scores = jnp.where(allowed, scores, NEG_FILL)
    row_max = jnp.max(scores, axis=-1, keepdims=True)
    weights = jnp.where(allowed, jnp.exp(scores - row_max), 0.0)
    total = jnp.sum(weights, axis=-1, keepdims=True)
    accum = jnp.einsum(
        "hqk,kd->hqd", weights.astype(bf16), value_all, preferred_element_type=jnp.float32
    )
    log_total = row_max + jnp.log(total)
    attn_heads = jnp.transpose(accum / total, (1, 0, 2)).astype(bf16)
    attn_out = attn_heads.reshape(rows, HEADS * HEAD)
    projected = matmul(attn_out, out_full)
    inv_proj = inverse_rms(projected)
    residual = inputs_f + projected * inv_proj * gain_attn
    inv_two = inverse_rms(residual)
    normed_two = (residual * inv_two * gain_pre).astype(bf16)

    (rows_all,) = exchange((normed_two,), ("gather",), "ctx", ctx, 2)
    rows_all = rows_all.reshape(-1, width)
    gate = matmul(rows_all, gate_full)
    upper = matmul(rows_all, up_full)
    gelu_val, gelu_der = gelu_pair(gate)
    hidden = (gelu_val * upper).astype(bf16)
    ffn_part = matmul_nt(hidden, down_full).astype(bf16).reshape(ctx, rows, width)
    (ffn_parts,) = exchange((ffn_part,), ("swap",), "ctx", ctx, 3)
    ffn_sum = sum_blocks(ffn_parts)
    inv_ffn = inverse_rms(ffn_sum)
    block_out = (residual + ffn_sum * inv_ffn * gain_post).astype(bf16)
    cot = cotangent.astype(jnp.float32)
    grad_post = jnp.sum(cot * ffn_sum * inv_ffn, axis=0)
    ffn_sum_grad = norm_back(ffn_sum, inv_ffn, gain_post, cot).astype(bf16)

    (grad_all,) = exchange((ffn_sum_grad,), ("gather",), "ctx", ctx, 4)
    grad_all = grad_all.reshape(-1, width)
    down_shard = lax.psum_scatter(
        matmul_tn(grad_all, hidden).astype(bf16), "dp", scatter_dimension=0, tiled=True
    ).astype(jnp.float32)
    hidden_grad = matmul(grad_all, down_full)
    gate_grad = (hidden_grad * upper * gelu_der).astype(bf16)
    up_grad = (hidden_grad * gelu_val).astype(bf16)
    gate_shard = lax.psum_scatter(
        matmul_tn(rows_all, gate_grad).astype(bf16), "dp", scatter_dimension=0, tiled=True
    ).astype(jnp.float32)
    up_shard = lax.psum_scatter(
        matmul_tn(rows_all, up_grad).astype(bf16), "dp", scatter_dimension=0, tiled=True
    ).astype(jnp.float32)
    two_part = (matmul_nt(gate_grad, gate_full) + matmul_nt(up_grad, up_full)).astype(bf16)
    two_parts, attn_all = exchange(
        (two_part.reshape(ctx, rows, width), attn_out), ("swap", "gather"), "ctx", ctx, 5
    )
    normed_two_grad = sum_blocks(two_parts)
    attn_all = attn_all.reshape(-1, attn_out.shape[1])
    grad_pre = jnp.sum(normed_two_grad * residual * inv_two, axis=0)
    residual_grad = cot + norm_back(residual, inv_two, gain_pre, normed_two_grad)
    grad_attn = jnp.sum(residual_grad * projected * inv_proj, axis=0)
    projected_grad = norm_back(projected, inv_proj, gain_attn, residual_grad).astype(bf16)
    attn_out_grad = matmul_nt(projected_grad, out_full).astype(bf16).reshape(rows, HEADS, HEAD)
    delta = jnp.sum(attn_out_grad.astype(jnp.float32) * attn_heads.astype(jnp.float32), axis=-1)
    delta = jnp.transpose(delta, (1, 0))[:, :, None]
    probs = jnp.where(allowed, jnp.exp(scores - log_total), 0.0)
    prob_grad = jnp.einsum(
        "qhd,kd->hqk", attn_out_grad, value_all, preferred_element_type=jnp.float32
    )
    score_grad = (probs * (prob_grad - delta)).astype(bf16)
    values_part = jnp.einsum(
        "hqk,qhd->kd", probs.astype(bf16), attn_out_grad, preferred_element_type=jnp.float32
    )
    keys_part = jnp.einsum("hqk,qhd->kd", score_grad, query_rot, preferred_element_type=jnp.float32)
    query_rot_grad = jnp.einsum(
        "hqk,kd->qhd", score_grad, key_all, preferred_element_type=jnp.float32
    )
    keys_parts, values_parts = exchange(
        (
            keys_part.astype(bf16).reshape(ctx, rows, kwidth),
            values_part.astype(bf16).reshape(ctx, rows, kwidth),
        ),
        ("swap", "swap"),
        "ctx",
        ctx,
        6,
    )
    key_rot_grad = sum_blocks(keys_parts)
    value_grad = sum_blocks(values_parts).astype(bf16)
    query_normed_grad = unrotate(query_rot_grad * scaling, cosine[:, None, :], sine[:, None, :])
    grad_qgain = jnp.sum(query_normed_grad * queries * inv_query, axis=(0, 1))
    query_grad = (
        norm_back(queries, inv_query, gain_query, query_normed_grad)
        .reshape(rows, HEADS * HEAD)
        .astype(bf16)
    )
    key_normed_grad = unrotate(key_rot_grad, cosine, sine)
    grad_kgain = jnp.sum(key_normed_grad * keys * inv_key, axis=0)
    key_grad = norm_back(keys, inv_key, gain_key, key_normed_grad).astype(bf16)
    mixed_grad = jnp.concatenate([query_grad, key_grad, value_grad], axis=1)
    normed_one_grad = matmul_nt(mixed_grad, mixed_full)
    grad_in = jnp.sum(normed_one_grad * inputs_f * inv_one, axis=0)
    input_grad = residual_grad + norm_back(inputs_f, inv_one, gain_in, normed_one_grad)

    gain_grads = (grad_in, grad_qgain, grad_kgain, grad_attn, grad_pre, grad_post)
    packed = jnp.concatenate([grad.reshape(dp, -1) for grad in gain_grads], axis=1)
    mixed_cols, out_cols, gain_parts = exchange(
        (by_columns(mixed_grad, ctx), by_columns(projected_grad, ctx), by_columns(packed, ctx)),
        ("swap",) * 3,
        "ctx",
        ctx,
        7,
    )
    mixed_w = matmul_tn(normed_all, mixed_cols.reshape(-1, mixed_columns)).astype(bf16)
    out_w = matmul_tn(attn_all, out_cols.reshape(-1, out_columns)).astype(bf16)
    mixed_w, out_w, gain_parts = exchange(
        (
            mixed_w.reshape(dp, -1, mixed_columns),
            out_w.reshape(dp, -1, out_columns),
            sum_blocks(gain_parts)[:, None],
        ),
        ("swap",) * 3,
        "dp",
        dp,
        8,
    )
    mixed_w, out_w, gain_parts = exchange(
        (sum_blocks(mixed_w).astype(bf16), sum_blocks(out_w).astype(bf16), sum_blocks(gain_parts)),
        ("gather",) * 3,
        "ctx",
        ctx,
        9,
    )
    mixed_w = from_columns(mixed_w).astype(jnp.float32)
    out_w = from_columns(out_w).astype(jnp.float32)
    gain_done = gain_parts.reshape(-1)
    share = [gain_done[low:high] for low, high in zip(cuts[:-1], cuts[1:])]
    return (
        block_out,
        input_grad,
        share[0],
        mixed_w[:, :qwidth],
        mixed_w[:, qwidth : qwidth + kwidth],
        mixed_w[:, qwidth + kwidth :],
        share[1],
        share[2],
        out_w,
        share[3],
        share[4],
        gate_shard,
        up_shard,
        down_shard,
        share[5],
    )


def solution(mesh):
    return jax.shard_map(
        functools.partial(on_device, mesh.shape["dp"], mesh.shape["ctx"]),
        mesh=mesh,
        in_specs=(
            P(("dp", "ctx"), None),
            P("dp"),
            P("dp", None),
            P("dp", None),
            P("dp", None),
            P("dp"),
            P("dp"),
            P("dp", None),
            P("dp"),
            P("dp"),
            P("dp", "ctx"),
            P("dp", "ctx"),
            P("dp", "ctx"),
            P("dp"),
            P(("dp", "ctx"), None),
        ),
        out_specs=(
            P(("dp", "ctx"), None),
            P(("dp", "ctx"), None),
            P("dp"),
            P("dp", None),
            P("dp", None),
            P("dp", None),
            P("dp"),
            P("dp"),
            P("dp", None),
            P("dp"),
            P("dp"),
            P("dp", "ctx"),
            P("dp", "ctx"),
            P("dp", "ctx"),
            P("dp"),
        ),
        check_vma=False,
    )
```

```python
import functools
import math

import jax
import jax.numpy as jnp
from jax import lax
from jax.experimental import pallas as pl
from jax.experimental.pallas import tpu as pltpu
from jax.sharding import PartitionSpec as P

HEADS = 4
HEAD = 256


EPS = 1e-06
GELU_C = math.sqrt(2.0 / math.pi)
NEG_FILL = -1e30


def inverse_rms(values):
    return lax.rsqrt(jnp.mean(values * values, axis=-1, keepdims=True) + EPS)


def norm_back(values, scale_inv, gain, grad_out):
    weighted = grad_out * gain
    cubed = scale_inv * scale_inv * scale_inv
    return scale_inv * weighted - values * cubed * jnp.mean(
        weighted * values, axis=-1, keepdims=True
    )


def gelu_pair(values):
    inner = GELU_C * (values + 0.044715 * values * values * values)
    tanh_val = jnp.tanh(inner)
    result = 0.5 * values * (1.0 + tanh_val)
    slope = 0.5 * (1.0 + tanh_val) + 0.5 * values * (1.0 - tanh_val * tanh_val) * GELU_C * (
        1.0 + 3.0 * 0.044715 * values * values
    )
    return (result, slope)


def rotate(values, cosine, sine):
    middle = values.shape[-1] // 2
    first = values[..., :middle]
    second = values[..., middle:]
    return jnp.concatenate(
        [first * cosine - second * sine, second * cosine + first * sine], axis=-1
    )


def unrotate(grads, cosine, sine):
    middle = grads.shape[-1] // 2
    first = grads[..., :middle]
    second = grads[..., middle:]
    return jnp.concatenate(
        [first * cosine + second * sine, second * cosine - first * sine], axis=-1
    )


def rope_tables(positions):
    middle = HEAD // 2
    freqs = jnp.exp(-(2.0 * jnp.arange(middle, dtype=jnp.float32) / HEAD) * math.log(1000000.0))
    angles = positions[:, None] * freqs[None, :]
    return (jnp.cos(angles), jnp.sin(angles))


def matmul(left, right):
    return jnp.dot(left, right, preferred_element_type=jnp.float32)


def matmul_tn(left, right):
    return lax.dot_general(
        left, right, (((0,), (0,)), ((), ())), preferred_element_type=jnp.float32
    )


def matmul_nt(left, right):
    return lax.dot_general(
        left, right, (((1,), (1,)), ((), ())), preferred_element_type=jnp.float32
    )


MESH = pl.DeviceIdType.MESH


def swap_kernel(size, axis, kinds, *refs):
    count = len(kinds)
    ins, outs, kept = refs[:count], refs[count : 2 * count], refs[2 * count : 3 * count]
    send, recv, local = refs[3 * count :]
    me = lax.axis_index(axis)
    own = []
    for item, kind in enumerate(kinds):
        source = ins[item].at[me] if kind == "swap" else ins[item]
        own.append(pltpu.make_async_copy(source, kept[item], local.at[item, 0]))
        own[-1].start()
    barrier = pltpu.get_barrier_semaphore()
    for step in range(1, size):
        peer = lax.rem(me + step, size)
        pl.semaphore_signal(barrier, inc=1, device_id={axis: peer}, device_id_type=MESH)
    pl.semaphore_wait(barrier, size - 1)
    copies = []
    for item, kind in enumerate(kinds):
        for step in range(1, size):
            peer = lax.rem(me + step, size)
            source = ins[item].at[peer] if kind == "swap" else ins[item]
            copy = pltpu.make_async_remote_copy(
                src_ref=source,
                dst_ref=outs[item].at[me],
                send_sem=send.at[item, step - 1],
                recv_sem=recv.at[item, step - 1],
                device_id={axis: peer},
                device_id_type=MESH,
            )
            copy.start()
            copies.append(copy)
    for item in range(count):
        own[item].wait()
        copy = pltpu.make_async_copy(kept[item], outs[item].at[me], local.at[item, 1])
        copy.start()
        copies.append(copy)
    for copy in copies:
        copy.wait()


def chunks_of(rows):
    for parts in (4, 3, 2):
        if rows % (16 * parts) == 0:
            return parts
    return 1


def pair_gather_kernel(size, axis, kinds, *refs):
    count = len(kinds)
    ins, outs, kept = refs[:count], refs[count : 2 * count], refs[2 * count : 3 * count]
    send, recv, pass_send, pass_recv, local = refs[3 * count :]
    me = lax.axis_index(axis)
    twin = me + 1 - 2 * lax.rem(me, 2)
    half = size // 2
    own = []
    for item in range(count):
        own.append(pltpu.make_async_copy(ins[item], kept[item], local.at[item, 0]))
        own[-1].start()
    barrier = pltpu.get_barrier_semaphore()
    for step in range(1, half):
        peer = lax.rem(me + 2 * step, size)
        pl.semaphore_signal(barrier, inc=1, device_id={axis: peer}, device_id_type=MESH)
    pl.semaphore_signal(barrier, inc=1, device_id={axis: twin}, device_id_type=MESH)
    pl.semaphore_wait(barrier, half)
    pieces = []
    for item in range(count):
        rows = ins[item].shape[0]
        pieces += [
            (item, part, pl.ds(part * (rows // chunks_of(rows)), rows // chunks_of(rows)))
            for part in range(chunks_of(rows))
        ]
    across, last = [], []
    for item, part, span in pieces:
        for step in range(1, half):
            copy = pltpu.make_async_remote_copy(
                src_ref=ins[item].at[span],
                dst_ref=outs[item].at[me, span],
                send_sem=send.at[item, step, part],
                recv_sem=recv.at[item, step, part],
                device_id={axis: lax.rem(me + 2 * step, size)},
                device_id_type=MESH,
            )
            copy.start()
            across.append((copy, item, step, part, span))
    for item, part, span in pieces:
        copy = pltpu.make_async_remote_copy(
            src_ref=ins[item].at[span],
            dst_ref=outs[item].at[me, span],
            send_sem=pass_send.at[item, 0, part],
            recv_sem=pass_recv.at[item, 0, part],
            device_id={axis: twin},
            device_id_type=MESH,
        )
        copy.start()
        last.append(copy)
    for item in range(count):
        own[item].wait()
        copy = pltpu.make_async_copy(kept[item], outs[item].at[me], local.at[item, 1])
        copy.start()
        last.append(copy)
    for arrived, item, step, part, span in across:
        arrived.wait_recv()
        origin = lax.rem(me + size - 2 * step, size)
        copy = pltpu.make_async_remote_copy(
            src_ref=outs[item].at[origin, span],
            dst_ref=outs[item].at[origin, span],
            send_sem=pass_send.at[item, step, part],
            recv_sem=pass_recv.at[item, step, part],
            device_id={axis: twin},
            device_id_type=MESH,
        )
        copy.start()
        last.append(copy)
    for sent, *_ in across:
        sent.wait_send()
    for copy in last:
        copy.wait()


def exchange(arrays, kinds, axis, size, ident):
    count = len(arrays)
    pairs = all(kind == "gather" for kind in kinds) and axis == "ctx" and size % 2 == 0
    shapes = tuple(
        jax.ShapeDtypeStruct(x.shape if kind == "swap" else (size,) + x.shape, x.dtype)
        for x, kind in zip(arrays, kinds)
    )
    dma = pltpu.SemaphoreType.DMA
    if pairs:
        half = size // 2
        parts = max(chunks_of(x.shape[0]) for x in arrays)
        scratch = [dma((count, half, parts))] * 4
        body = pair_gather_kernel
    else:
        scratch = [dma((count, size - 1))] * 2
        body = swap_kernel
    moved = sum(x.size * x.dtype.itemsize for x in shapes)
    return pl.pallas_call(
        functools.partial(body, size, axis, tuple(kinds)),
        out_shape=shapes,
        in_specs=[pl.BlockSpec(memory_space=pl.ANY)] * count,
        out_specs=tuple(pl.BlockSpec(memory_space=pl.ANY) for _ in arrays),
        scratch_shapes=[pltpu.VMEM(x.shape[1:], x.dtype) for x in shapes]
        + scratch
        + [dma((count, 2))],
        compiler_params=pltpu.CompilerParams(collective_id=ident, has_side_effects=True),
        cost_estimate=pl.CostEstimate(flops=0, bytes_accessed=20 * moved, transcendentals=0),
        name=f"exchange_{ident}",
    )(*arrays)


def by_columns(array, parts):
    rows, columns = array.shape
    return jnp.transpose(array.reshape(rows, parts, columns // parts), (1, 0, 2))


def from_columns(array):
    parts, rows, columns = array.shape
    return jnp.transpose(array, (1, 0, 2)).reshape(rows, parts * columns)


def sum_blocks(array):
    return jnp.sum(array.astype(jnp.float32), axis=0)


def on_device(
    dp,
    ctx,
    tokens,
    in_gain,
    query_weight,
    key_weight,
    value_weight,
    query_gain,
    key_gain,
    out_weight,
    attn_post_gain,
    ffn_pre_gain,
    gate_weight,
    up_weight,
    down_weight,
    ffn_post_gain,
    cotangent,
):
    rows, width = tokens.shape
    bf16 = jnp.bfloat16
    scaling = 1.0 / math.sqrt(HEAD)
    ctx_index = lax.axis_index("ctx")
    query_pos = ctx_index * rows + jnp.arange(rows, dtype=jnp.int32)
    cosine, sine = rope_tables(query_pos.astype(jnp.float32))

    mixed = jnp.concatenate([query_weight, key_weight, value_weight], axis=1)
    mixed_columns = mixed.shape[1] // ctx
    out_columns = out_weight.shape[1] // ctx
    mixed_slice = lax.dynamic_slice_in_dim(mixed, ctx_index * mixed_columns, mixed_columns, 1)
    out_slice = lax.dynamic_slice_in_dim(out_weight, ctx_index * out_columns, out_columns, 1)
    gains = (in_gain, query_gain, key_gain, attn_post_gain, ffn_pre_gain, ffn_post_gain)
    cuts = [0]
    for gain in gains:
        cuts.append(cuts[-1] + gain.shape[0])
    packed_gains = jnp.concatenate([gain.astype(jnp.float32) for gain in gains])[None]
    mixed_dp, out_dp, gains_dp = exchange(
        (mixed_slice, out_slice, packed_gains), ("gather",) * 3, "dp", dp, 0
    )
    gate_weight, up_weight, down_weight, mixed_dp = lax.optimization_barrier(
        (gate_weight, up_weight, down_weight, mixed_dp)
    )
    gate_full, up_full, down_full = (
        lax.all_gather(gate_weight, "dp", axis=0, tiled=True),
        lax.all_gather(up_weight, "dp", axis=0, tiled=True),
        lax.all_gather(down_weight, "dp", axis=0, tiled=True),
    )
    gains_dp = gains_dp[:, 0]
    gain_in, gain_query, gain_key, gain_attn, gain_pre, gain_post = (
        gains_dp[:, low:high].reshape(-1) for low, high in zip(cuts[:-1], cuts[1:])
    )
    mixed_all, out_all, tokens_all = exchange(
        (
            mixed_dp.reshape(-1, mixed_columns),
            out_dp.reshape(-1, out_columns),
            tokens,
        ),
        ("gather",) * 3,
        "ctx",
        ctx,
        1,
    )
    mixed_full = from_columns(mixed_all)
    out_full = from_columns(out_all)
    qwidth = query_weight.shape[1]
    kwidth = key_weight.shape[1]
    query_full = mixed_full[:, :qwidth]
    key_full = mixed_full[:, qwidth : qwidth + kwidth]
    value_full = mixed_full[:, qwidth + kwidth :]

    inputs_f = tokens.astype(jnp.float32)
    inv_one = inverse_rms(inputs_f)
    normed_one = (inputs_f * inv_one * gain_in).astype(bf16)
    all_f = tokens_all.reshape(-1, width).astype(jnp.float32)
    normed_all = (all_f * inverse_rms(all_f) * gain_in).astype(bf16)
    key_pos = jnp.arange(all_f.shape[0], dtype=jnp.int32)
    cosine_all, sine_all = rope_tables(key_pos.astype(jnp.float32))
    queries = matmul(normed_one, query_full).reshape(rows, HEADS, HEAD)
    keys = matmul(normed_one, key_full)
    keys_every = matmul(normed_all, key_full)
    value_all = matmul(normed_all, value_full).astype(bf16)
    inv_query = inverse_rms(queries)
    inv_key = inverse_rms(keys)
    query_rot = (
        rotate(queries * inv_query * gain_query, cosine[:, None, :], sine[:, None, :]) * scaling
    ).astype(bf16)
    key_all = rotate(
        keys_every * inverse_rms(keys_every) * gain_key, cosine_all, sine_all
    ).astype(bf16)
    allowed = (query_pos[:, None] >= key_pos[None, :])[None]
    scores = jnp.einsum("qhd,kd->hqk", query_rot, key_all, preferred_element_type=jnp.float32)
    scores = jnp.where(allowed, scores, NEG_FILL)
    row_max = jnp.max(scores, axis=-1, keepdims=True)
    weights = jnp.where(allowed, jnp.exp(scores - row_max), 0.0)
    total = jnp.sum(weights, axis=-1, keepdims=True)
    accum = jnp.einsum(
        "hqk,kd->hqd", weights.astype(bf16), value_all, preferred_element_type=jnp.float32
    )
    log_total = row_max + jnp.log(total)
    attn_heads = jnp.transpose(accum / total, (1, 0, 2)).astype(bf16)
    attn_out = attn_heads.reshape(rows, HEADS * HEAD)
    projected = matmul(attn_out, out_full)
    inv_proj = inverse_rms(projected)
    residual = inputs_f + projected * inv_proj * gain_attn
    inv_two = inverse_rms(residual)
    normed_two = (residual * inv_two * gain_pre).astype(bf16)

    attn_all = lax.all_gather(attn_out, "ctx", axis=0, tiled=True)
    (rows_all,) = exchange((normed_two,), ("gather",), "ctx", ctx, 2)
    rows_all = rows_all.reshape(-1, width)
    gate = matmul(rows_all, gate_full)
    upper = matmul(rows_all, up_full)
    gelu_val, gelu_der = gelu_pair(gate)
    hidden = (gelu_val * upper).astype(bf16)
    ffn_part = matmul_nt(hidden, down_full).astype(bf16).reshape(ctx, rows, width)
    (ffn_parts,) = exchange((ffn_part,), ("swap",), "ctx", ctx, 3)
    ffn_sum = sum_blocks(ffn_parts)
    inv_ffn = inverse_rms(ffn_sum)
    block_out = (residual + ffn_sum * inv_ffn * gain_post).astype(bf16)
    cot = cotangent.astype(jnp.float32)
    grad_post = jnp.sum(cot * ffn_sum * inv_ffn, axis=0)
    ffn_sum_grad = norm_back(ffn_sum, inv_ffn, gain_post, cot).astype(bf16)

    (grad_all,) = exchange((ffn_sum_grad,), ("gather",), "ctx", ctx, 4)
    grad_all, attn_all = lax.optimization_barrier((grad_all.reshape(-1, width), attn_all))
    down_shard = lax.psum_scatter(
        matmul_tn(grad_all, hidden).astype(bf16), "dp", scatter_dimension=0, tiled=True
    ).astype(jnp.float32)
    hidden_grad = matmul(grad_all, down_full)
    gate_grad = (hidden_grad * upper * gelu_der).astype(bf16)
    up_grad = (hidden_grad * gelu_val).astype(bf16)
    two_part, gate_part, up_part = lax.optimization_barrier(
        (
            (matmul_nt(gate_grad, gate_full) + matmul_nt(up_grad, up_full)).astype(bf16),
            matmul_tn(rows_all, gate_grad).astype(bf16),
            matmul_tn(rows_all, up_grad).astype(bf16),
        )
    )
    gate_shard = lax.psum_scatter(gate_part, "dp", scatter_dimension=0, tiled=True)
    gate_shard = gate_shard.astype(jnp.float32)
    up_shard = lax.psum_scatter(up_part, "dp", scatter_dimension=0, tiled=True)
    up_shard = up_shard.astype(jnp.float32)
    (two_parts,) = exchange((two_part.reshape(ctx, rows, width),), ("swap",), "ctx", ctx, 5)
    normed_two_grad = sum_blocks(two_parts)
    grad_pre = jnp.sum(normed_two_grad * residual * inv_two, axis=0)
    residual_grad = cot + norm_back(residual, inv_two, gain_pre, normed_two_grad)
    grad_attn = jnp.sum(residual_grad * projected * inv_proj, axis=0)
    projected_grad = norm_back(projected, inv_proj, gain_attn, residual_grad).astype(bf16)
    attn_out_grad = matmul_nt(projected_grad, out_full).astype(bf16).reshape(rows, HEADS, HEAD)
    delta = jnp.sum(attn_out_grad.astype(jnp.float32) * attn_heads.astype(jnp.float32), axis=-1)
    delta = jnp.transpose(delta, (1, 0))[:, :, None]
    probs = jnp.where(allowed, jnp.exp(scores - log_total), 0.0)
    prob_grad = jnp.einsum(
        "qhd,kd->hqk", attn_out_grad, value_all, preferred_element_type=jnp.float32
    )
    score_grad = (probs * (prob_grad - delta)).astype(bf16)
    values_part = jnp.einsum(
        "hqk,qhd->kd", probs.astype(bf16), attn_out_grad, preferred_element_type=jnp.float32
    )
    keys_part = jnp.einsum("hqk,qhd->kd", score_grad, query_rot, preferred_element_type=jnp.float32)
    query_rot_grad = jnp.einsum(
        "hqk,kd->qhd", score_grad, key_all, preferred_element_type=jnp.float32
    )
    keys_parts, values_parts = exchange(
        (
            keys_part.astype(bf16).reshape(ctx, rows, kwidth),
            values_part.astype(bf16).reshape(ctx, rows, kwidth),
        ),
        ("swap", "swap"),
        "ctx",
        ctx,
        6,
    )
    key_rot_grad = sum_blocks(keys_parts)
    value_grad = sum_blocks(values_parts).astype(bf16)
    query_normed_grad = unrotate(query_rot_grad * scaling, cosine[:, None, :], sine[:, None, :])
    grad_qgain = jnp.sum(query_normed_grad * queries * inv_query, axis=(0, 1))
    query_grad = (
        norm_back(queries, inv_query, gain_query, query_normed_grad)
        .reshape(rows, HEADS * HEAD)
        .astype(bf16)
    )
    key_normed_grad = unrotate(key_rot_grad, cosine, sine)
    grad_kgain = jnp.sum(key_normed_grad * keys * inv_key, axis=0)
    key_grad = norm_back(keys, inv_key, gain_key, key_normed_grad).astype(bf16)
    mixed_grad = jnp.concatenate([query_grad, key_grad, value_grad], axis=1)
    normed_one_grad = matmul_nt(mixed_grad, mixed_full)
    grad_in = jnp.sum(normed_one_grad * inputs_f * inv_one, axis=0)
    input_grad = residual_grad + norm_back(inputs_f, inv_one, gain_in, normed_one_grad)

    gain_grads = (grad_in, grad_qgain, grad_kgain, grad_attn, grad_pre, grad_post)
    packed = jnp.concatenate([grad.reshape(dp, -1) for grad in gain_grads], axis=1)
    mixed_cols, out_cols, gain_parts = exchange(
        (by_columns(mixed_grad, ctx), by_columns(projected_grad, ctx), by_columns(packed, ctx)),
        ("swap",) * 3,
        "ctx",
        ctx,
        7,
    )
    mixed_w = matmul_tn(normed_all, mixed_cols.reshape(-1, mixed_columns)).astype(bf16)
    out_w = matmul_tn(attn_all, out_cols.reshape(-1, out_columns)).astype(bf16)
    mixed_w, out_w, gain_parts = exchange(
        (
            mixed_w.reshape(dp, -1, mixed_columns),
            out_w.reshape(dp, -1, out_columns),
            sum_blocks(gain_parts)[:, None],
        ),
        ("swap",) * 3,
        "dp",
        dp,
        8,
    )
    mixed_w, out_w, gain_parts = exchange(
        (sum_blocks(mixed_w).astype(bf16), sum_blocks(out_w).astype(bf16), sum_blocks(gain_parts)),
        ("gather",) * 3,
        "ctx",
        ctx,
        9,
    )
    mixed_w = from_columns(mixed_w).astype(jnp.float32)
    out_w = from_columns(out_w).astype(jnp.float32)
    gain_done = gain_parts.reshape(-1)
    share = [gain_done[low:high] for low, high in zip(cuts[:-1], cuts[1:])]
    return (
        block_out,
        input_grad,
        share[0],
        mixed_w[:, :qwidth],
        mixed_w[:, qwidth : qwidth + kwidth],
        mixed_w[:, qwidth + kwidth :],
        share[1],
        share[2],
        out_w,
        share[3],
        share[4],
        gate_shard,
        up_shard,
        down_shard,
        share[5],
    )


def solution(mesh):
    return jax.shard_map(
        functools.partial(on_device, mesh.shape["dp"], mesh.shape["ctx"]),
        mesh=mesh,
        in_specs=(
            P(("dp", "ctx"), None),
            P("dp"),
            P("dp", None),
            P("dp", None),
            P("dp", None),
            P("dp"),
            P("dp"),
            P("dp", None),
            P("dp"),
            P("dp"),
            P("dp", "ctx"),
            P("dp", "ctx"),
            P("dp", "ctx"),
            P("dp"),
            P(("dp", "ctx"), None),
        ),
        out_specs=(
            P(("dp", "ctx"), None),
            P(("dp", "ctx"), None),
            P("dp"),
            P("dp", None),
            P("dp", None),
            P("dp", None),
            P("dp"),
            P("dp"),
            P("dp", None),
            P("dp"),
            P("dp"),
            P("dp", "ctx"),
            P("dp", "ctx"),
            P("dp", "ctx"),
            P("dp"),
        ),
        check_vma=False,
    )
```

```python
import functools
import math

import jax
import jax.numpy as jnp
from jax import lax
from jax.experimental import pallas as pl
from jax.experimental.pallas import tpu as pltpu
from jax.sharding import PartitionSpec as P

HEADS = 4
HEAD = 256


EPS = 1e-06
GELU_C = math.sqrt(2.0 / math.pi)
NEG_FILL = -1e30


def inverse_rms(values):
    return lax.rsqrt(jnp.mean(values * values, axis=-1, keepdims=True) + EPS)


def norm_back(values, scale_inv, gain, grad_out):
    weighted = grad_out * gain
    cubed = scale_inv * scale_inv * scale_inv
    return scale_inv * weighted - values * cubed * jnp.mean(
        weighted * values, axis=-1, keepdims=True
    )


def gelu_pair(values):
    inner = GELU_C * (values + 0.044715 * values * values * values)
    tanh_val = jnp.tanh(inner)
    result = 0.5 * values * (1.0 + tanh_val)
    slope = 0.5 * (1.0 + tanh_val) + 0.5 * values * (1.0 - tanh_val * tanh_val) * GELU_C * (
        1.0 + 3.0 * 0.044715 * values * values
    )
    return (result, slope)


def rotate(values, cosine, sine):
    middle = values.shape[-1] // 2
    first = values[..., :middle]
    second = values[..., middle:]
    return jnp.concatenate(
        [first * cosine - second * sine, second * cosine + first * sine], axis=-1
    )


def unrotate(grads, cosine, sine):
    middle = grads.shape[-1] // 2
    first = grads[..., :middle]
    second = grads[..., middle:]
    return jnp.concatenate(
        [first * cosine + second * sine, second * cosine - first * sine], axis=-1
    )


def rope_tables(positions):
    middle = HEAD // 2
    freqs = jnp.exp(-(2.0 * jnp.arange(middle, dtype=jnp.float32) / HEAD) * math.log(1000000.0))
    angles = positions[:, None] * freqs[None, :]
    return (jnp.cos(angles), jnp.sin(angles))


def matmul(left, right):
    return jnp.dot(left, right, preferred_element_type=jnp.float32)


def matmul_tn(left, right):
    return lax.dot_general(
        left, right, (((0,), (0,)), ((), ())), preferred_element_type=jnp.float32
    )


def matmul_nt(left, right):
    return lax.dot_general(
        left, right, (((1,), (1,)), ((), ())), preferred_element_type=jnp.float32
    )


MESH = pl.DeviceIdType.MESH


def swap_kernel(size, axis, kinds, *refs):
    count = len(kinds)
    ins, outs, kept = refs[:count], refs[count : 2 * count], refs[2 * count : 3 * count]
    send, recv, local = refs[3 * count :]
    me = lax.axis_index(axis)
    own = []
    for item, kind in enumerate(kinds):
        source = ins[item].at[me] if kind == "swap" else ins[item]
        own.append(pltpu.make_async_copy(source, kept[item], local.at[item, 0]))
        own[-1].start()
    barrier = pltpu.get_barrier_semaphore()
    for step in range(1, size):
        peer = lax.rem(me + step, size)
        pl.semaphore_signal(barrier, inc=1, device_id={axis: peer}, device_id_type=MESH)
    pl.semaphore_wait(barrier, size - 1)
    copies = []
    for item, kind in enumerate(kinds):
        for step in range(1, size):
            peer = lax.rem(me + step, size)
            source = ins[item].at[peer] if kind == "swap" else ins[item]
            copy = pltpu.make_async_remote_copy(
                src_ref=source,
                dst_ref=outs[item].at[me],
                send_sem=send.at[item, step - 1],
                recv_sem=recv.at[item, step - 1],
                device_id={axis: peer},
                device_id_type=MESH,
            )
            copy.start()
            copies.append(copy)
    for item in range(count):
        own[item].wait()
        copy = pltpu.make_async_copy(kept[item], outs[item].at[me], local.at[item, 1])
        copy.start()
        copies.append(copy)
    for copy in copies:
        copy.wait()


def chunks_of(rows):
    for parts in (4, 3, 2):
        if rows % (16 * parts) == 0:
            return parts
    return 1


def pair_gather_kernel(size, axis, kinds, *refs):
    count = len(kinds)
    ins, outs, kept = refs[:count], refs[count : 2 * count], refs[2 * count : 3 * count]
    send, recv, pass_send, pass_recv, local = refs[3 * count :]
    me = lax.axis_index(axis)
    twin = me + 1 - 2 * lax.rem(me, 2)
    half = size // 2
    own = []
    for item in range(count):
        own.append(pltpu.make_async_copy(ins[item], kept[item], local.at[item, 0]))
        own[-1].start()
    barrier = pltpu.get_barrier_semaphore()
    for step in range(1, half):
        peer = lax.rem(me + 2 * step, size)
        pl.semaphore_signal(barrier, inc=1, device_id={axis: peer}, device_id_type=MESH)
    pl.semaphore_signal(barrier, inc=1, device_id={axis: twin}, device_id_type=MESH)
    pl.semaphore_wait(barrier, half)
    pieces = []
    for item in range(count):
        rows = ins[item].shape[0]
        pieces += [
            (item, part, pl.ds(part * (rows // chunks_of(rows)), rows // chunks_of(rows)))
            for part in range(chunks_of(rows))
        ]
    across, last = [], []
    for item, part, span in pieces:
        for step in range(1, half):
            copy = pltpu.make_async_remote_copy(
                src_ref=ins[item].at[span],
                dst_ref=outs[item].at[me, span],
                send_sem=send.at[item, step, part],
                recv_sem=recv.at[item, step, part],
                device_id={axis: lax.rem(me + 2 * step, size)},
                device_id_type=MESH,
            )
            copy.start()
            across.append((copy, item, step, part, span))
    for item, part, span in pieces:
        copy = pltpu.make_async_remote_copy(
            src_ref=ins[item].at[span],
            dst_ref=outs[item].at[me, span],
            send_sem=pass_send.at[item, 0, part],
            recv_sem=pass_recv.at[item, 0, part],
            device_id={axis: twin},
            device_id_type=MESH,
        )
        copy.start()
        last.append(copy)
    for item in range(count):
        own[item].wait()
        copy = pltpu.make_async_copy(kept[item], outs[item].at[me], local.at[item, 1])
        copy.start()
        last.append(copy)
    for arrived, item, step, part, span in across:
        arrived.wait_recv()
        origin = lax.rem(me + size - 2 * step, size)
        copy = pltpu.make_async_remote_copy(
            src_ref=outs[item].at[origin, span],
            dst_ref=outs[item].at[origin, span],
            send_sem=pass_send.at[item, step, part],
            recv_sem=pass_recv.at[item, step, part],
            device_id={axis: twin},
            device_id_type=MESH,
        )
        copy.start()
        last.append(copy)
    for sent, *_ in across:
        sent.wait_send()
    for copy in last:
        copy.wait()


def exchange(arrays, kinds, axis, size, ident):
    count = len(arrays)
    pairs = all(kind == "gather" for kind in kinds) and axis == "ctx" and size % 2 == 0
    shapes = tuple(
        jax.ShapeDtypeStruct(x.shape if kind == "swap" else (size,) + x.shape, x.dtype)
        for x, kind in zip(arrays, kinds)
    )
    dma = pltpu.SemaphoreType.DMA
    if pairs:
        half = size // 2
        parts = max(chunks_of(x.shape[0]) for x in arrays)
        scratch = [dma((count, half, parts))] * 4
        body = pair_gather_kernel
    else:
        scratch = [dma((count, size - 1))] * 2
        body = swap_kernel
    moved = sum(x.size * x.dtype.itemsize for x in shapes)
    return pl.pallas_call(
        functools.partial(body, size, axis, tuple(kinds)),
        out_shape=shapes,
        in_specs=[pl.BlockSpec(memory_space=pl.ANY)] * count,
        out_specs=tuple(pl.BlockSpec(memory_space=pl.ANY) for _ in arrays),
        scratch_shapes=[pltpu.VMEM(x.shape[1:], x.dtype) for x in shapes]
        + scratch
        + [dma((count, 2))],
        compiler_params=pltpu.CompilerParams(collective_id=ident, has_side_effects=True),
        cost_estimate=pl.CostEstimate(flops=0, bytes_accessed=20 * moved, transcendentals=0),
        name=f"exchange_{ident}",
    )(*arrays)


def by_columns(array, parts):
    rows, columns = array.shape
    return jnp.transpose(array.reshape(rows, parts, columns // parts), (1, 0, 2))


def from_columns(array):
    parts, rows, columns = array.shape
    return jnp.transpose(array, (1, 0, 2)).reshape(rows, parts * columns)


def sum_blocks(array):
    return jnp.sum(array.astype(jnp.float32), axis=0)


def on_device(
    dp,
    ctx,
    tokens,
    in_gain,
    query_weight,
    key_weight,
    value_weight,
    query_gain,
    key_gain,
    out_weight,
    attn_post_gain,
    ffn_pre_gain,
    gate_weight,
    up_weight,
    down_weight,
    ffn_post_gain,
    cotangent,
):
    rows, width = tokens.shape
    bf16 = jnp.bfloat16
    scaling = 1.0 / math.sqrt(HEAD)
    ctx_index = lax.axis_index("ctx")
    query_pos = ctx_index * rows + jnp.arange(rows, dtype=jnp.int32)
    cosine, sine = rope_tables(query_pos.astype(jnp.float32))

    qwidth = query_weight.shape[1]
    kwidth = key_weight.shape[1]
    mixed_columns = (qwidth + 2 * kwidth) // ctx
    out_columns = out_weight.shape[1] // ctx
    query_columns = qwidth // ctx
    pair = jnp.concatenate([key_weight, value_weight], axis=1)
    pair_rows = pair.shape[0] // ctx
    out_rows = out_weight.shape[0] // ctx
    query_slice = lax.dynamic_slice_in_dim(query_weight, ctx_index * query_columns, query_columns, 1)
    pair_slice = lax.dynamic_slice_in_dim(pair, ctx_index * pair_rows, pair_rows, 0)
    out_slice = lax.dynamic_slice_in_dim(out_weight, ctx_index * out_rows, out_rows, 0)
    gains = (in_gain, query_gain, key_gain, attn_post_gain, ffn_pre_gain, ffn_post_gain)
    cuts = [0]
    for gain in gains:
        cuts.append(cuts[-1] + gain.shape[0])
    packed_gains = jnp.concatenate([gain.astype(jnp.float32) for gain in gains])[None]
    query_dp, pair_dp, out_dp, gains_dp = exchange(
        (query_slice, pair_slice, out_slice, packed_gains), ("gather",) * 4, "dp", dp, 0
    )
    gate_weight, up_weight, down_weight, query_dp = lax.optimization_barrier(
        (gate_weight, up_weight, down_weight, query_dp)
    )
    gate_full, up_full, down_full = (
        lax.all_gather(gate_weight, "dp", axis=0, tiled=True),
        lax.all_gather(up_weight, "dp", axis=0, tiled=True),
        lax.all_gather(down_weight, "dp", axis=0, tiled=True),
    )
    gains_dp = gains_dp[:, 0]
    gain_in, gain_query, gain_key, gain_attn, gain_pre, gain_post = (
        gains_dp[:, low:high].reshape(-1) for low, high in zip(cuts[:-1], cuts[1:])
    )
    query_all, pair_all, out_all, tokens_all = exchange(
        (query_dp.reshape(-1, query_columns), pair_dp, out_dp, tokens),
        ("gather",) * 4,
        "ctx",
        ctx,
        1,
    )
    query_full = from_columns(query_all)
    pair_full = jnp.transpose(pair_all, (1, 0, 2, 3)).reshape(-1, 2 * kwidth)
    key_full = pair_full[:, :kwidth]
    value_full = pair_full[:, kwidth:]
    out_full = jnp.transpose(out_all, (1, 0, 2, 3)).reshape(-1, out_weight.shape[1])

    inputs_f = tokens.astype(jnp.float32)
    inv_one = inverse_rms(inputs_f)
    normed_one = (inputs_f * inv_one * gain_in).astype(bf16)
    all_f = tokens_all.reshape(-1, width).astype(jnp.float32)
    normed_all = (all_f * inverse_rms(all_f) * gain_in).astype(bf16)
    key_pos = jnp.arange(all_f.shape[0], dtype=jnp.int32)
    cosine_all, sine_all = rope_tables(key_pos.astype(jnp.float32))
    queries = matmul(normed_one, query_full).reshape(rows, HEADS, HEAD)
    keys = matmul(normed_one, key_full)
    keys_every = matmul(normed_all, key_full)
    value_all = matmul(normed_all, value_full).astype(bf16)
    inv_query = inverse_rms(queries)
    inv_key = inverse_rms(keys)
    query_rot = (
        rotate(queries * inv_query * gain_query, cosine[:, None, :], sine[:, None, :]) * scaling
    ).astype(bf16)
    key_all = rotate(
        keys_every * inverse_rms(keys_every) * gain_key, cosine_all, sine_all
    ).astype(bf16)
    allowed = (query_pos[:, None] >= key_pos[None, :])[None]
    scores = jnp.einsum("qhd,kd->hqk", query_rot, key_all, preferred_element_type=jnp.float32)
    scores = jnp.where(allowed, scores, NEG_FILL)
    row_max = jnp.max(scores, axis=-1, keepdims=True)
    weights = jnp.where(allowed, jnp.exp(scores - row_max), 0.0)
    total = jnp.sum(weights, axis=-1, keepdims=True)
    accum = jnp.einsum(
        "hqk,kd->hqd", weights.astype(bf16), value_all, preferred_element_type=jnp.float32
    )
    log_total = row_max + jnp.log(total)
    attn_heads = jnp.transpose(accum / total, (1, 0, 2)).astype(bf16)
    attn_out = attn_heads.reshape(rows, HEADS * HEAD)
    projected = matmul(attn_out, out_full)
    inv_proj = inverse_rms(projected)
    residual = inputs_f + projected * inv_proj * gain_attn
    inv_two = inverse_rms(residual)
    normed_two = (residual * inv_two * gain_pre).astype(bf16)

    attn_all = lax.all_gather(attn_out, "ctx", axis=0, tiled=True)
    (rows_all,) = exchange((normed_two,), ("gather",), "ctx", ctx, 2)
    rows_all = rows_all.reshape(-1, width)
    gate = matmul(rows_all, gate_full)
    upper = matmul(rows_all, up_full)
    gelu_val, gelu_der = gelu_pair(gate)
    hidden = (gelu_val * upper).astype(bf16)
    ffn_part = matmul_nt(hidden, down_full).astype(bf16).reshape(ctx, rows, width)
    (ffn_parts,) = exchange((ffn_part,), ("swap",), "ctx", ctx, 3)
    ffn_sum = sum_blocks(ffn_parts)
    inv_ffn = inverse_rms(ffn_sum)
    block_out = (residual + ffn_sum * inv_ffn * gain_post).astype(bf16)
    cot = cotangent.astype(jnp.float32)
    grad_post = jnp.sum(cot * ffn_sum * inv_ffn, axis=0)
    ffn_sum_grad = norm_back(ffn_sum, inv_ffn, gain_post, cot).astype(bf16)

    (grad_all,) = exchange((ffn_sum_grad,), ("gather",), "ctx", ctx, 4)
    grad_all, attn_all = lax.optimization_barrier((grad_all.reshape(-1, width), attn_all))
    down_part, grad_all = lax.optimization_barrier(
        (matmul_tn(grad_all, hidden).astype(bf16), grad_all)
    )
    down_shard = lax.psum_scatter(down_part, "dp", scatter_dimension=0, tiled=True)
    down_shard = down_shard.astype(jnp.float32)
    hidden_grad = matmul(grad_all, down_full)
    gate_grad = (hidden_grad * upper * gelu_der).astype(bf16)
    up_grad = (hidden_grad * gelu_val).astype(bf16)
    two_part, gate_part, up_part = lax.optimization_barrier(
        (
            (matmul_nt(gate_grad, gate_full) + matmul_nt(up_grad, up_full)).astype(bf16),
            matmul_tn(rows_all, gate_grad).astype(bf16),
            matmul_tn(rows_all, up_grad).astype(bf16),
        )
    )
    gate_shard = lax.psum_scatter(gate_part, "dp", scatter_dimension=0, tiled=True)
    gate_shard = gate_shard.astype(jnp.float32)
    up_shard = lax.psum_scatter(up_part, "dp", scatter_dimension=0, tiled=True)
    up_shard = up_shard.astype(jnp.float32)
    (two_parts,) = exchange((two_part.reshape(ctx, rows, width),), ("swap",), "ctx", ctx, 5)
    normed_two_grad = sum_blocks(two_parts)
    grad_pre = jnp.sum(normed_two_grad * residual * inv_two, axis=0)
    residual_grad = cot + norm_back(residual, inv_two, gain_pre, normed_two_grad)
    grad_attn = jnp.sum(residual_grad * projected * inv_proj, axis=0)
    projected_grad = norm_back(projected, inv_proj, gain_attn, residual_grad).astype(bf16)
    attn_out_grad = matmul_nt(projected_grad, out_full).astype(bf16).reshape(rows, HEADS, HEAD)
    delta = jnp.sum(attn_out_grad.astype(jnp.float32) * attn_heads.astype(jnp.float32), axis=-1)
    delta = jnp.transpose(delta, (1, 0))[:, :, None]
    probs = jnp.where(allowed, jnp.exp(scores - log_total), 0.0)
    prob_grad = jnp.einsum(
        "qhd,kd->hqk", attn_out_grad, value_all, preferred_element_type=jnp.float32
    )
    score_grad = (probs * (prob_grad - delta)).astype(bf16)
    values_part = jnp.einsum(
        "hqk,qhd->kd", probs.astype(bf16), attn_out_grad, preferred_element_type=jnp.float32
    )
    keys_part = jnp.einsum("hqk,qhd->kd", score_grad, query_rot, preferred_element_type=jnp.float32)
    query_rot_grad = jnp.einsum(
        "hqk,kd->qhd", score_grad, key_all, preferred_element_type=jnp.float32
    )
    keys_parts, values_parts = exchange(
        (
            keys_part.astype(bf16).reshape(ctx, rows, kwidth),
            values_part.astype(bf16).reshape(ctx, rows, kwidth),
        ),
        ("swap", "swap"),
        "ctx",
        ctx,
        6,
    )
    key_rot_grad = sum_blocks(keys_parts)
    value_grad = sum_blocks(values_parts).astype(bf16)
    query_normed_grad = unrotate(query_rot_grad * scaling, cosine[:, None, :], sine[:, None, :])
    grad_qgain = jnp.sum(query_normed_grad * queries * inv_query, axis=(0, 1))
    query_grad = (
        norm_back(queries, inv_query, gain_query, query_normed_grad)
        .reshape(rows, HEADS * HEAD)
        .astype(bf16)
    )
    key_normed_grad = unrotate(key_rot_grad, cosine, sine)
    grad_kgain = jnp.sum(key_normed_grad * keys * inv_key, axis=0)
    key_grad = norm_back(keys, inv_key, gain_key, key_normed_grad).astype(bf16)
    mixed_grad = jnp.concatenate([query_grad, key_grad, value_grad], axis=1)
    normed_one_grad = matmul_nt(query_grad, query_full) + matmul_nt(
        mixed_grad[:, qwidth:], pair_full
    )
    grad_in = jnp.sum(normed_one_grad * inputs_f * inv_one, axis=0)
    input_grad = residual_grad + norm_back(inputs_f, inv_one, gain_in, normed_one_grad)

    gain_grads = (grad_in, grad_qgain, grad_kgain, grad_attn, grad_pre, grad_post)
    packed = jnp.concatenate([grad.reshape(dp, -1) for grad in gain_grads], axis=1)
    both = jnp.concatenate([by_columns(mixed_grad, ctx), by_columns(projected_grad, ctx)], axis=2)
    both, gain_parts = exchange(
        (both, by_columns(packed, ctx)),
        ("swap",) * 2,
        "ctx",
        ctx,
        7,
    )
    mixed_w = matmul_tn(normed_all, both[:, :, :mixed_columns].reshape(-1, mixed_columns)).astype(bf16)
    out_w = matmul_tn(attn_all, both[:, :, mixed_columns:].reshape(-1, out_columns)).astype(bf16)
    mixed_w, out_w, gain_parts = exchange(
        (
            mixed_w.reshape(dp, -1, mixed_columns),
            out_w.reshape(dp, -1, out_columns),
            sum_blocks(gain_parts)[:, None],
        ),
        ("swap",) * 3,
        "dp",
        dp,
        8,
    )
    mixed_w, out_w, gain_parts = exchange(
        (sum_blocks(mixed_w).astype(bf16), sum_blocks(out_w).astype(bf16), sum_blocks(gain_parts)),
        ("gather",) * 3,
        "ctx",
        ctx,
        9,
    )
    mixed_w = from_columns(mixed_w).astype(jnp.float32)
    out_w = from_columns(out_w).astype(jnp.float32)
    gain_done = gain_parts.reshape(-1)
    share = [gain_done[low:high] for low, high in zip(cuts[:-1], cuts[1:])]
    return (
        block_out,
        input_grad,
        share[0],
        mixed_w[:, :qwidth],
        mixed_w[:, qwidth : qwidth + kwidth],
        mixed_w[:, qwidth + kwidth :],
        share[1],
        share[2],
        out_w,
        share[3],
        share[4],
        gate_shard,
        up_shard,
        down_shard,
        share[5],
    )


def solution(mesh):
    return jax.shard_map(
        functools.partial(on_device, mesh.shape["dp"], mesh.shape["ctx"]),
        mesh=mesh,
        in_specs=(
            P(("dp", "ctx"), None),
            P("dp"),
            P("dp", None),
            P("dp", None),
            P("dp", None),
            P("dp"),
            P("dp"),
            P("dp", None),
            P("dp"),
            P("dp"),
            P("dp", "ctx"),
            P("dp", "ctx"),
            P("dp", "ctx"),
            P("dp"),
            P(("dp", "ctx"), None),
        ),
        out_specs=(
            P(("dp", "ctx"), None),
            P(("dp", "ctx"), None),
            P("dp"),
            P("dp", None),
            P("dp", None),
            P("dp", None),
            P("dp"),
            P("dp"),
            P("dp", None),
            P("dp"),
            P("dp"),
            P("dp", "ctx"),
            P("dp", "ctx"),
            P("dp", "ctx"),
            P("dp"),
        ),
        check_vma=False,
    )
```
